256 devices in a mesh: blk: 32 (over y, z_lo, core), grp: 8 (over z_hi, x).
Axes of the slice: x: 4, y: 4, z: 8 (z_hi: 2, z_lo: 4; z = z_hi * 4 + z_lo), core: 2. Of those that a mesh axis runs over, the one named last changes fastest.
Arguments:
- samples: float32 [128, 256, 256], P('blk', 'grp'), may hold values from -11 to 11
- pair_table: int32 [128, 16], P('blk'), may hold values from 0 to 127
- assignment: int32 [2, 128], P(None, 'blk'), may hold values from 0 to 255
- band_index: int32 [2], replicated, may hold values from 0 to 1023
Outputs:
- log_weight: float32 [2, 128, 256], P(None, 'blk', 'grp')
The draws below stay inside these ranges and needn't reach their ends.
All inputs are finite; a program needn't handle non-finite values.
Results may differ from the reference program's by a relative error of at most 0.0003.
Values sent between devices are 32-bit elements; how exact they have to be, the bound alone decides.
A program may use at most 128 MiB of HBM per device.

```python
import math
import jax
import jax.numpy as jnp
import numpy as np
from jax import lax

D = 256
ITERS = 2
PAIRS = 16
M = 128
S = 256


def draw_samples(key, part):
    keys_all = jax.random.split(jax.random.fold_in(key, 11), 7)
    noise = jnp.clip(jax.random.normal(keys_all[0], (M, S, D), jnp.float32), -4.0, 4.0)
    chosen = jax.random.randint(keys_all[4], (), 0, M)
    picked = (jax.random.uniform(keys_all[5], (M,), jnp.float32) < 0.25) | (jnp.arange(M) == chosen)
    sign = jnp.where(jax.random.uniform(keys_all[6], (M,), jnp.float32) < 0.5, -1.0, 1.0)
    shift = jnp.where(picked, 6.5 * sign, 0.0)[:, None, None]
    offsets = jax.random.uniform(keys_all[1], (M, 1, D), jnp.float32, -0.5, 0.5)
    return jnp.clip(offsets + noise + shift, -11.0, 11.0)


def set_ends(drawn, key, smallest, largest):
    dims = drawn.shape
    place = [jax.random.randint(jax.random.fold_in(key, axis), (), 0, dims[axis]) for axis in range(len(dims))]
    drawn = drawn.at[tuple(place)].set(smallest)
    longest = dims.index(max(dims))
    place[longest] = (place[longest] + 1) % dims[longest]
    return drawn.at[tuple(place)].set(largest)


def rank_table(amount, slope):
    loads = [(1 << 20) // math.isqrt(rank ** slope) + 1 for rank in range(1, amount + 1)]
    deviation = 1 + sum(loads) // (1 << 30)
    return np.cumsum(np.array([max(1, weight // deviation) for weight in loads]))


def ranked(own_key, dims, amount, slope):
    grid = rank_table(amount, slope)
    ticket = jax.random.randint(jax.random.fold_in(own_key, 1), dims, 0, int(grid[amount - 1]))
    grade = jnp.searchsorted(jnp.asarray(grid, jnp.int32), ticket, side="right")
    return jax.random.permutation(jax.random.fold_in(own_key, 2), amount)[grade].astype(jnp.int32)


def setup_inputs(seed: int = 0) -> dict:
    keys = jax.random.split(jax.random.key(seed), 5)
    samples = draw_samples(jax.random.fold_in(keys[4], 71), 0)
    pair_table = set_ends(ranked(keys[1], (M, PAIRS), M, 2), jax.random.fold_in(keys[1], 3), 0, M - 1).astype(jnp.int32)
    assignment = set_ends(jax.random.randint(keys[2], (ITERS, M), 0, S), jax.random.fold_in(keys[2], 1), 0, S - 1).astype(jnp.int32)
    band_index = jax.random.randint(keys[3], (ITERS,), 0, 1024).astype(jnp.int32)
    return {"samples": samples, "pair_table": pair_table, "assignment": assignment, "band_index": band_index}


def reference(samples, pair_table, assignment, band_index):
    band_sq = D * (1.0 + band_index.astype(jnp.float32) / 256.0) / 32.0
    flat = samples.reshape(M * S, D)
    flat_norm = jnp.sum(flat * flat, -1)
    members = jnp.arange(M, dtype=jnp.int32)
    picked = samples[members[None, :], assignment]
    centre = jnp.sum(picked, axis=1) / M
    counts = jnp.sum((pair_table[:, :, None] == members[None, None, :]).astype(jnp.float32), axis=1)

    def per_member(member):
        query = lax.dynamic_index_in_dim(samples, member, 0, keepdims=False)
        query_norm = jnp.sum(query * query, -1)
        product = jnp.einsum("qd,kd->qk", query, flat, precision=lax.Precision.HIGHEST)
        distance = query_norm[:, None] + flat_norm[None, :] - 2.0 * product
        stacked = []
        for turn in range(ITERS):
            scores = (-distance / (2.0 * band_sq[turn])).reshape(S, M, S)
            peak = jnp.max(scores, -1)
            stacked.append(peak + jnp.log(jnp.sum(jnp.exp(scores - peak[..., None]), -1)))
        return jnp.stack(stacked)

    kernel = lax.map(per_member, members)
    weighted = jnp.einsum("atsm,am->tas", kernel, counts, precision=lax.Precision.HIGHEST) / PAIRS
    spread = samples[None] - centre[:, None, None, :]
    logits = weighted - jnp.sum(spread * spread, -1) / (2.0 * band_sq[:, None, None])
    peak = jnp.max(logits, -1, keepdims=True)
    totals = jnp.sum(jnp.exp(logits - peak), -1, keepdims=True)
    return logits - peak - jnp.log(totals)
```

```python
import functools
import math

import jax
import jax.numpy as jnp
from jax import lax
from jax.experimental import pallas as pl
from jax.experimental.pallas import tpu as pltpu
from jax.sharding import Mesh
from jax.sharding import PartitionSpec as P

MESH = pl.DeviceIdType.MESH
NAMES = ("y", "zl", "core", "zh", "x")
Y, ZL, CORES, ZH, X = 4, 4, 2, 2, 4
GROUP = ZH * X
SUBS, ROWS, D, ROUNDS, PAIRS, MEMBERS = 4, 32, 256, 2, 16, 128
DRAWS = GROUP * ROWS
TILES = SUBS * ROWS // 8 + 1
HALF = TILES // 2
LOG2E = math.log2(math.e)
LN2 = math.log(2.0)
NT = (((1,), (1,)), ((), ()))


def split(value):
    high = value.astype(jnp.bfloat16)
    low = (value - high.astype(jnp.float32)).astype(jnp.bfloat16)
    return high, low


def nt_dot(a, b):
    return lax.dot_general(a, b, NT, preferred_element_type=jnp.float32)


def row_sums(value):
    ones = jnp.ones((8, value.shape[1]), jnp.bfloat16)
    high, low = split(value)
    lowest = (value - high.astype(jnp.float32) - low.astype(jnp.float32)).astype(jnp.bfloat16)
    return (nt_dot(ones, high) + nt_dot(ones, low) + nt_dot(ones, lowest))[0:1]


def kernel(
    table, picks, bands, own, out,
    keys, queries, parts_hi, parts_lo, query_half, sums_out, sums_in, centre_out, centre_in, final_out, final_in,
    z_send, z_recv, y_send, y_recv, half_send, half_recv, sib_send, sib_recv,
    zh_send, zh_recv, x_send, x_recv, xhalf_send, xhalf_recv,
    c_send, c_recv, l_send, l_recv, f_send, f_recv,
):
    y, zl, core, zh, x = (lax.axis_index(name) for name in NAMES)
    me = zh * X + x

    def block(row, seg):
        return (row * ZL + seg) * CORES + core

    def device(**where):
        return where

    def copy(src, dst, send, recv, **where):
        made = pltpu.make_async_remote_copy(
            src_ref=src, dst_ref=dst, send_sem=send, recv_sem=recv, device_id=where, device_id_type=MESH
        )
        return made

    y_up, y_down = lax.rem(y + 1, Y), lax.rem(y + Y - 1, Y)
    x_up, x_down = lax.rem(x + 1, X), lax.rem(x + X - 1, X)
    segs = [lax.rem(zl + k, ZL) for k in range(ZL)]
    others = [(dz, dx) for dx in range(X) for dz in range(ZH) if (dz, dx) != (0, 0)]

    def peer(dz, dx):
        return lax.rem(zh + dz, ZH), lax.rem(x + dx, X)

    barrier = pltpu.get_barrier_semaphore()
    greeted = [{"zl": segs[k]} for k in range(1, ZL)]
    greeted += [{"y": y_up}, {"y": y_down}, {"core": 1 - core}]
    for dz, dx in others:
        to_zh, to_x = peer(dz, dx)
        greeted.append({"zh": to_zh, "x": to_x})
    for where in greeted:
        pl.semaphore_signal(barrier, inc=1, device_id=where, device_id_type=MESH)

    mine = block(y, zl)
    held = own[...]
    keys[mine, 0 : TILES - 1] = held.reshape(TILES - 1, 8, D)
    queries[me] = held
    number = lax.broadcasted_iota(jnp.int32, (ROWS, D), 0)
    chosen = []
    for t in range(ROUNDS):
        total = jnp.zeros((ROWS, D), jnp.float32)
        for m in range(SUBS):
            total += jnp.where(number == picks[t, m] - me * ROWS, held[m], 0.0)
        chosen.append(jnp.sum(total, 0, keepdims=True))
    line = lax.broadcasted_iota(jnp.int32, (8, D), 0)
    keys[mine, TILES - 1] = jnp.where(line == 0, chosen[0], jnp.where(line == 1, chosen[1], 0.0))

    pl.semaphore_wait(barrier, len(greeted))

    sends = []

    def go(made):
        made.start()
        sends.append(made)
        return made

    z_copies, y_copies, half_copies, sib_copies = [], {}, {}, []

    def to_sibling(b):
        n = len(sib_copies)
        sib_copies.append(
            go(copy(keys.at[b], keys.at[b], sib_send.at[n], sib_recv.at[n], core=1 - core))
        )

    def along_y(k):
        b = block(y, segs[k])
        for side, to in enumerate((y_up, y_down)):
            y_copies[k, side] = go(copy(keys.at[b], keys.at[b], y_send.at[k, side], y_recv.at[k, side], y=to))

    def along_y_again(k):
        for side, (source, to) in enumerate(((y_down, y_up), (y_up, y_down))):
            b = block(source, segs[k])
            y_copies[k, side].wait_recv()
            part = pl.ds(0, HALF) if side == 0 else pl.ds(HALF, TILES - HALF)
            half_copies[k, side] = go(
                copy(
                    keys.at[b, part], keys.at[b, part], half_send.at[k, side], half_recv.at[k, side], y=to
                )
            )
            to_sibling(b)

    along_y(0)
    for k in range(1, ZL):
        z_copies.append(
            go(copy(keys.at[mine], keys.at[mine], z_send.at[k - 1], z_recv.at[k - 1], zl=segs[k]))
        )
    zh_copy = go(copy(queries.at[me], queries.at[me], zh_send, zh_recv, zh=1 - zh))
    x_copies, xhalf_copies = {}, {}

    def along_x(k):
        slot = lax.rem(zh + k, ZH) * X + x
        for side, to in enumerate((x_up, x_down)):
            x_copies[k, side] = go(
                copy(queries.at[slot], queries.at[slot], x_send.at[k, side], x_recv.at[k, side], x=to)
            )

    def along_x_again(k):
        for side, (source, to) in enumerate(((x_down, x_up), (x_up, x_down))):
            slot = lax.rem(zh + k, ZH) * X + source
            x_copies[k, side].wait_recv()
            part = pl.ds(0, SUBS // 2) if side == 0 else pl.ds(SUBS // 2, SUBS // 2)
            xhalf_copies[k, side] = go(
                copy(
                    queries.at[slot, part], queries.at[slot, part],
                    xhalf_send.at[k, side], xhalf_recv.at[k, side], x=to,
                )
            )

    along_x(0)
    to_sibling(mine)

    def z_arrived(k):
        z_copies[k - 1].wait_recv()

    back = [lax.rem(zl + ZL - k, ZL) for k in range(ZL)]
    segs = back
    along_y_again(0)
    along_x_again(0)
    z_arrived(1)
    along_y(1)
    to_sibling(block(y, segs[1]))
    zh_copy.wait_recv()
    along_x(1)
    z_arrived(2)
    along_y(2)
    to_sibling(block(y, segs[2]))
    along_y_again(1)
    z_arrived(3)
    along_y(3)
    to_sibling(block(y, segs[3]))
    along_x_again(1)
    along_y_again(2)

    for made in xhalf_copies.values():
        made.wait_recv()
    for m in range(SUBS):
        whole = queries[:, m].reshape(DRAWS, D)
        high, low = split(whole)
        parts_hi[m] = high
        parts_lo[m] = low
        query_half[m] = jnp.broadcast_to(0.5 * row_sums(whole * whole), (8, DRAWS))

    along_y_again(3)
    far = lax.rem(y + 2, Y)
    for k in range(ZL):
        half_copies[k, 0].wait_recv()
        half_copies[k, 1].wait_recv()
        to_sibling(block(far, segs[k]))
    for made in sib_copies:
        made.wait_recv()

    total = keys[0, TILES - 1]
    for b in range(1, Y * ZL * CORES):
        total += keys[b, TILES - 1]
    centre_out[...] = total
    centre_in[me] = total
    c_copies = []
    for n, (dz, dx) in enumerate(others):
        to_zh, to_x = peer(dz, dx)
        c_copies.append(go(copy(centre_out, centre_in.at[me], c_send.at[n], c_recv.at[n], zh=to_zh, x=to_x)))

    scale = []
    for t in range(ROUNDS):
        index = jnp.full((1, DRAWS), bands[t], jnp.int32).astype(jnp.float32)
        scale.append((D / 32.0) * (1.0 + index / 256.0))

    l_copies = []
    slots = 8
    for k in range(X):
        m = lax.rem(x + 1 + k, X)
        high, low = parts_hi[m], parts_lo[m]
        shift = query_half[m, 0:1]
        for first in range(0, PAIRS, slots):
            rows = []
            for s in range(first, first + slots):
                p = table[m, s]
                b = lax.div(p, SUBS)
                q = lax.rem(p, SUBS) * (ROWS // 8)
                rows.append(keys[b, pl.ds(q, ROWS // 8)].reshape(ROWS, D))
            rows = jnp.concatenate(rows, 0)
            norm_half = 0.5 * jnp.sum(rows * rows, -1, keepdims=True)
            key_high, key_low = split(rows)
            product = nt_dot(key_high, high) + nt_dot(key_low, high) + nt_dot(key_high, low)
            value = (product - norm_half).reshape(slots, ROWS, DRAWS)
            peak = jnp.max(value, 1, keepdims=True)
            value = value - peak
            peak = peak.reshape(slots, DRAWS) - shift
            for t in range(ROUNDS):
                rate = LOG2E / scale[t]
                mass = jnp.sum(jnp.exp2(value * rate[None]), 1)
                sums_out[m, t, pl.ds(first, slots)] = peak * rate + jnp.log2(mass)
        for dz in range(ZH):
            if (dz, k) == (0, X - 1):
                sums_in[me] = sums_out[m, zh]
                continue
            n = len(l_copies)
            to_zh = lax.rem(zh + dz, ZH)
            l_copies.append(
                go(
                    copy(
                        sums_out.at[m, to_zh], sums_in.at[me], l_send.at[n], l_recv.at[n], zh=to_zh, x=m
                    )
                )
            )

    for made in c_copies:
        made.wait_recv()
    centre = jnp.sum(centre_in[:, pl.ds(zh, 1)].reshape(GROUP, D), 0, keepdims=True) / MEMBERS
    away = queries[:, x].reshape(DRAWS, D) - centre
    spread = row_sums(away * away)
    band = jnp.where(zh == 0, scale[0], scale[1])
    for made in l_copies:
        made.wait_recv()
    pieces = sums_in[...]
    peak = jnp.max(pieces, 0)
    whole = peak + jnp.log2(jnp.sum(jnp.exp2(pieces - peak[None]), 0))
    logits = (LN2 / PAIRS) * jnp.sum(whole, 0, keepdims=True) - spread / (2.0 * band)
    logits = logits - jnp.max(logits, -1, keepdims=True)
    result = logits - jnp.log(jnp.sum(jnp.exp(logits), -1, keepdims=True))
    for g in range(GROUP):
        final_out[g, 0:1, 0:ROWS] = result[:, g * ROWS : (g + 1) * ROWS]
    f_copies = []
    for n, (dz, dx) in enumerate(others):
        to_zh, to_x = peer(dz, dx)
        f_copies.append(
            go(
                copy(
                    final_out.at[to_zh * X + to_x], final_in.at[me], f_send.at[n], f_recv.at[n],
                    zh=to_zh, x=to_x,
                )
            )
        )
    final_in[me] = final_out[me]
    for made in f_copies:
        made.wait_recv()
    out[...] = final_in[:, 0, 0:ROWS].reshape(ROUNDS, SUBS, ROWS)
    for made in sends:
        made.wait_send()


def per_device(samples, pair_table, assignment, band_index):
    dma = pltpu.SemaphoreType.DMA
    smem = pl.BlockSpec(memory_space=pltpu.SMEM)
    vmem = pl.BlockSpec(memory_space=pltpu.VMEM)
    f32 = jnp.float32
    peers = GROUP - 1
    return pl.pallas_call(
        kernel,
        name="weights",
        out_shape=jax.ShapeDtypeStruct((ROUNDS, SUBS, ROWS), f32),
        in_specs=[smem, smem, smem, vmem],
        out_specs=vmem,
        scratch_shapes=[
            pltpu.VMEM((Y * ZL * CORES, TILES, 8, D), f32),
            pltpu.VMEM((GROUP, SUBS, ROWS, D), f32),
            pltpu.VMEM((SUBS, DRAWS, D), jnp.bfloat16),
            pltpu.VMEM((SUBS, DRAWS, D), jnp.bfloat16),
            pltpu.VMEM((SUBS, 8, DRAWS), f32),
            pltpu.VMEM((SUBS, ROUNDS, PAIRS, DRAWS), f32),
            pltpu.VMEM((GROUP, PAIRS, DRAWS), f32),
            pltpu.VMEM((8, D), f32),
            pltpu.VMEM((GROUP, 8, D), f32),
            pltpu.VMEM((GROUP, 8, 128), f32),
            pltpu.VMEM((GROUP, 8, 128), f32),
            dma((ZL - 1,)), dma((ZL - 1,)),
            dma((ZL, 2)), dma((ZL, 2)),
            dma((ZL, 2)), dma((ZL, 2)),
            dma((Y * ZL,)), dma((Y * ZL,)),
            dma, dma,
            dma((ZH, 2)), dma((ZH, 2)),
            dma((ZH, 2)), dma((ZH, 2)),
            dma((peers,)), dma((peers,)),
            dma((peers,)), dma((peers,)),
            dma((peers,)), dma((peers,)),
        ],
        compiler_params=pltpu.CompilerParams(
            collective_id=0, has_side_effects=True, vmem_limit_bytes=48 * 1024 * 1024
        ),
    )(pair_table, assignment, band_index, samples)


def solution(mesh):
    finer = Mesh(mesh.devices.reshape(Y, ZL, CORES, ZH, X), NAMES)
    blk, grp = NAMES[:3], NAMES[3:]
    return jax.shard_map(
        per_device,
        mesh=finer,
        in_specs=(P(blk, grp, None), P(blk, None), P(None, blk), P()),
        out_specs=P(None, blk, grp),
        check_vma=False,
    )
```

```python
import math

import jax
import jax.numpy as jnp
from jax import lax
from jax.experimental import pallas as pl
from jax.experimental.pallas import tpu as pltpu
from jax.sharding import Mesh
from jax.sharding import PartitionSpec as P

MESH = pl.DeviceIdType.MESH
NAMES = ("y", "zl", "core", "zh", "x")
Y, ZL, CORES, ZH, X = 4, 4, 2, 2, 4
GROUP = ZH * X
SUBS, ROWS, D, ROUNDS, PAIRS, MEMBERS = 4, 32, 256, 2, 16, 128
DRAWS = GROUP * ROWS
HALF = SUBS // 2
SLOTS = 8
LOG2E = math.log2(math.e)
LN2 = math.log(2.0)
NT = (((1,), (1,)), ((), ()))


def split(value):
    high = value.astype(jnp.bfloat16)
    low = (value - high.astype(jnp.float32)).astype(jnp.bfloat16)
    return high, low


def nt_dot(a, b):
    return lax.dot_general(a, b, NT, preferred_element_type=jnp.float32)


def row_sums(value):
    ones = jnp.ones((8, value.shape[1]), jnp.bfloat16)
    high, low = split(value)
    lowest = (value - high.astype(jnp.float32) - low.astype(jnp.float32)).astype(jnp.bfloat16)
    return (nt_dot(ones, high) + nt_dot(ones, low) + nt_dot(ones, lowest))[0:1]


def log_sum(pieces):
    peak = jnp.max(pieces, 0)
    return peak + jnp.log2(jnp.sum(jnp.exp2(pieces - peak[None]), 0))


def kernel(
    table, picks, bands, own, out,
    keys, queries, parts_hi, parts_lo, query_half, sums_out, sums_in, pair_out, pair_in,
    pick_out, pick_in, final_out, final_in,
    z_send, z_recv, y_send, y_recv, half_send, half_recv, sib_send, sib_recv,
    zh_send, zh_recv, x_send, x_recv, xhalf_send, xhalf_recv,
    p_send, p_recv, l_send, l_recv, pair_send, pair_recv, f_send, f_recv,
):
    y, zl, core, zh, x = (lax.axis_index(name) for name in NAMES)
    me = zh * X + x

    def block(row, seg):
        return (row * ZL + seg) * CORES + core

    def copy(src, dst, send, recv, **where):
        return pltpu.make_async_remote_copy(
            src_ref=src, dst_ref=dst, send_sem=send, recv_sem=recv, device_id=where, device_id_type=MESH
        )

    y_up, y_down, y_far = (lax.rem(y + k, Y) for k in (1, 3, 2))
    x_up, x_down, x_far = (lax.rem(x + k, X) for k in (1, 3, 2))

    barrier = pltpu.get_barrier_semaphore()
    greeted = [{"core": 1 - core}, {"zh": 1 - zh}]
    greeted += [{"zl": lax.rem(zl + k, ZL)} for k in range(1, ZL)]
    greeted += [{"y": k} for k in (y_up, y_down, y_far)]
    greeted += [{"x": k} for k in (x_up, x_down, x_far)]
    for where in greeted:
        pl.semaphore_signal(barrier, inc=1, device_id=where, device_id_type=MESH)

    mine = block(y, zl)
    held = own[...]
    keys[mine] = held
    queries[me] = held
    number = lax.broadcasted_iota(jnp.int32, (ROWS, D), 0)
    pick_out[0] = jnp.zeros((8, 128), jnp.float32)
    for t in range(ROUNDS):
        total = jnp.zeros((ROWS, D), jnp.float32)
        for m in range(SUBS):
            total += jnp.where(number == picks[t, m] - me * ROWS, held[m], 0.0)
        total = jnp.sum(total, 0, keepdims=True)
        for side in range(2):
            pick_out[0, 2 * t + side : 2 * t + side + 1] = total[:, 128 * side : 128 * side + 128]

    pl.semaphore_wait(barrier, len(greeted))

    sends = []

    def go(made):
        made.start()
        sends.append(made)
        return made

    low = zl < 2
    segs = [zl, zl + 1 - 2 * lax.rem(zl, 2), jnp.where(low, 2, 1), jnp.where(low, 3, 0)]
    y_copies, half_copies, sib_copies = {}, {}, []

    def to_sibling(*where):
        n = len(sib_copies)
        part = keys.at[where]
        sib_copies.append(go(copy(part, part, sib_send.at[n], sib_recv.at[n], core=1 - core)))

    def z_copy(seg, up):
        b = block(y, seg)
        return copy(
            keys.at[b], keys.at[b], z_send.at[seg, int(up)], z_recv.at[seg], zl=zl + 1 if up else zl - 1
        )

    def along_y(k):
        b = block(y, segs[k])
        for side, to in enumerate((y_up, y_down)):
            y_copies[k, side] = go(copy(keys.at[b], keys.at[b], y_send.at[k, side], y_recv.at[k, side], y=to))
        to_sibling(b)

    def along_y_again(k):
        for side, (source, to) in enumerate(((y_down, y_up), (y_up, y_down))):
            b = block(source, segs[k])
            y_copies[k, side].wait_recv()
            part = keys.at[b, pl.ds(side * HALF, HALF)]
            half_copies[k, side] = go(copy(part, part, half_send.at[k, side], half_recv.at[k, side], y=to))
            to_sibling(b)

    def far_arrived(k):
        for side in range(2):
            half_copies[k, side].wait_recv()
            to_sibling(block(y_far, segs[k]), pl.ds(side * HALF, HALF))

    def z_arrived(k):
        seg = segs[k]
        z_copy(seg, True).wait_recv()

        @pl.when((seg < zl) & (zl < ZL - 1))
        def _():
            z_copy(seg, True).start()

        @pl.when((seg > zl) & (zl > 0))
        def _():
            z_copy(seg, False).start()

    def z_sent(k):
        seg = segs[k]

        @pl.when((seg <= zl) & (zl < ZL - 1))
        def _():
            z_copy(seg, True).wait_send()

        @pl.when((seg >= zl) & (zl > 0))
        def _():
            z_copy(seg, False).wait_send()

    x_copies, xhalf_copies = {}, {}

    def along_x(k):
        slot = lax.rem(zh + k, ZH) * X + x
        for side, to in enumerate((x_up, x_down)):
            x_copies[k, side] = go(
                copy(queries.at[slot], queries.at[slot], x_send.at[k, side], x_recv.at[k, side], x=to)
            )

    def along_x_again(k):
        for side, (source, to) in enumerate(((x_down, x_up), (x_up, x_down))):
            slot = lax.rem(zh + k, ZH) * X + source
            x_copies[k, side].wait_recv()
            part = queries.at[slot, pl.ds(side * HALF, HALF)]
            xhalf_copies[k, side] = go(copy(part, part, xhalf_send.at[k, side], xhalf_recv.at[k, side], x=to))

    axes = [
        [{"core": 1 - core}],
        [{"zl": lax.rem(zl + k, ZL)} for k in range(1, ZL)],
        [{"y": lax.rem(y + k, Y)} for k in range(1, Y)],
        [{"x": lax.rem(x + k, X)} for k in range(1, X)],
        [{"zh": 1 - zh}],
    ]
    pick_copies = {}

    def picks_along(a):
        for n, where in enumerate(axes[a]):
            pick_copies[a, n] = go(
                copy(pick_out.at[a], pick_in.at[a, n], p_send.at[a, n], p_recv.at[a, n], **where)
            )

    def picks_arrived(a):
        total = pick_out[a]
        for n in range(len(axes[a])):
            pick_copies[a, n].wait_recv()
            total += pick_in[a, n]
        pick_out[a + 1] = total

    @pl.when(zl < ZL - 1)
    def _():
        z_copy(zl, True).start()

    @pl.when(zl > 0)
    def _():
        z_copy(zl, False).start()

    along_y(0)
    along_x(0)
    picks_along(0)
    picks_arrived(0)
    picks_along(1)
    z_arrived(1)
    along_y(1)
    zh_copy = go(copy(queries.at[me], queries.at[me], zh_send, zh_recv, zh=1 - zh))
    along_x_again(0)
    along_y_again(0)
    picks_arrived(1)
    picks_along(2)
    z_arrived(2)
    along_y(2)
    along_y_again(1)
    picks_arrived(2)
    picks_along(3)
    far_arrived(0)
    zh_copy.wait_recv()
    along_x(1)
    z_arrived(3)
    along_y(3)
    picks_arrived(3)
    picks_along(4)
    along_x_again(1)
    along_y_again(2)
    far_arrived(1)
    for k in range(ZH):
        for side in range(2):
            xhalf_copies[k, side].wait_recv()

    for m in range(SUBS):
        whole = queries[:, m].reshape(DRAWS, D)
        high, low = split(whole)
        parts_hi[m] = high
        parts_lo[m] = low
        query_half[m] = jnp.broadcast_to(0.5 * row_sums(whole * whole), (8, DRAWS))

    picks_arrived(4)
    along_y_again(3)
    far_arrived(2)

    band, spread = [], []
    for t in range(ROUNDS):
        index = jnp.full((1, DRAWS), bands[t], jnp.int32).astype(jnp.float32)
        band.append((D / 32.0) * (1.0 + index / 256.0))
        centre = jnp.concatenate([pick_out[5, 2 * t : 2 * t + 1], pick_out[5, 2 * t + 1 : 2 * t + 2]], 1)
        away = queries[:, x].reshape(DRAWS, D) - centre / MEMBERS
        spread.append(row_sums(away * away) / (2.0 * band[t]))

    far_arrived(3)
    for made in sib_copies:
        made.wait_recv()

    l_copies = []
    for n, m in enumerate((x_far, x_up, x_down, x)):
        high, low = parts_hi[m], parts_lo[m]
        shift = query_half[m, 0:1]
        for first in range(0, PAIRS, SLOTS):
            rows = []
            for s in range(first, first + SLOTS):
                p = table[m, s]
                rows.append(keys[lax.div(p, SUBS), lax.rem(p, SUBS)])
            rows = jnp.concatenate(rows, 0)
            norm_half = 0.5 * jnp.sum(rows * rows, -1, keepdims=True)
            key_high, key_low = split(rows)
            product = nt_dot(key_high, high) + nt_dot(key_low, high) + nt_dot(key_high, low)
            value = (product - norm_half).reshape(SLOTS, ROWS, DRAWS)
            peak = jnp.max(value, 1, keepdims=True)
            value = value - peak
            peak = peak.reshape(SLOTS, DRAWS) - shift
            for t in range(ROUNDS):
                rate = LOG2E / band[t]
                mass = jnp.sum(jnp.exp2(value * rate[None]), 1)
                sums_out[m, t, pl.ds(first, SLOTS)] = peak * rate + jnp.log2(mass)
        if n < X - 1:
            l_copies.append(go(copy(sums_out.at[m], sums_in.at[n], l_send.at[n], l_recv.at[n], x=m)))
        else:
            sums_in[n] = sums_out[m]

    for made in l_copies:
        made.wait_recv()
    pair_out[...] = log_sum(sums_in[...])
    pair_copy = go(copy(pair_out, pair_in, pair_send, pair_recv, zh=1 - zh))
    pair_copy.wait_recv()
    first, second = pair_out[...], pair_in[...]
    peak = jnp.maximum(first, second)
    whole = peak + jnp.log2(jnp.exp2(first - peak) + jnp.exp2(second - peak))
    for t in range(ROUNDS):
        logits = (LN2 / PAIRS) * jnp.sum(whole[t], 0, keepdims=True) - spread[t]
        logits = logits - jnp.max(logits, -1, keepdims=True)
        result = logits - jnp.log(jnp.sum(jnp.exp(logits), -1, keepdims=True))
        result = jnp.where(zh == 0, result[:, : X * ROWS], result[:, X * ROWS :])
        for k in range(X):
            final_out[k, t : t + 1, 0:ROWS] = result[:, k * ROWS : (k + 1) * ROWS]
    f_copies = []
    for n, k in enumerate((x_far, x_up, x_down)):
        f_copies.append(go(copy(final_out.at[k], final_in.at[x], f_send.at[n], f_recv.at[n], x=k)))
    final_in[x] = final_out[x]
    for made in f_copies:
        made.wait_recv()
    for m in range(SUBS):
        out[:, m] = final_in[m, 0:ROUNDS, 0:ROWS]
    for made in sends:
        made.wait_send()
    for k in range(ZL):
        z_sent(k)


def per_device(samples, pair_table, assignment, band_index):
    dma = pltpu.SemaphoreType.DMA
    smem = pl.BlockSpec(memory_space=pltpu.SMEM)
    vmem = pl.BlockSpec(memory_space=pltpu.VMEM)
    f32 = jnp.float32
    siblings = (Y + 1) * ZL
    return pl.pallas_call(
        kernel,
        name="weights",
        out_shape=jax.ShapeDtypeStruct((ROUNDS, SUBS, ROWS), f32),
        in_specs=[smem, smem, smem, vmem],
        out_specs=vmem,
        scratch_shapes=[
            pltpu.VMEM((Y * ZL * CORES, SUBS, ROWS, D), f32),
            pltpu.VMEM((GROUP, SUBS, ROWS, D), f32),
            pltpu.VMEM((SUBS, DRAWS, D), jnp.bfloat16),
            pltpu.VMEM((SUBS, DRAWS, D), jnp.bfloat16),
            pltpu.VMEM((SUBS, 8, DRAWS), f32),
            pltpu.VMEM((SUBS, ROUNDS, PAIRS, DRAWS), f32),
            pltpu.VMEM((X, ROUNDS, PAIRS, DRAWS), f32),
            pltpu.VMEM((ROUNDS, PAIRS, DRAWS), f32),
            pltpu.VMEM((ROUNDS, PAIRS, DRAWS), f32),
            pltpu.VMEM((6, 8, 128), f32),
            pltpu.VMEM((5, 3, 8, 128), f32),
            pltpu.VMEM((X, 8, 128), f32),
            pltpu.VMEM((X, 8, 128), f32),
            dma((ZL, 2)), dma((ZL,)),
            dma((ZL, 2)), dma((ZL, 2)),
            dma((ZL, 2)), dma((ZL, 2)),
            dma((siblings,)), dma((siblings,)),
            dma, dma,
            dma((ZH, 2)), dma((ZH, 2)),
            dma((ZH, 2)), dma((ZH, 2)),
            dma((5, 3)), dma((5, 3)),
            dma((X - 1,)), dma((X - 1,)),
            dma, dma,
            dma((X - 1,)), dma((X - 1,)),
        ],
        compiler_params=pltpu.CompilerParams(
            collective_id=0, has_side_effects=True, vmem_limit_bytes=48 * 1024 * 1024
        ),
    )(pair_table, assignment, band_index, samples)


def solution(mesh):
    finer = Mesh(mesh.devices.reshape(Y, ZL, CORES, ZH, X), NAMES)
    blk, grp = NAMES[:3], NAMES[3:]
    return jax.shard_map(
        per_device,
        mesh=finer,
        in_specs=(P(blk, grp, None), P(blk, None), P(None, blk), P()),
        out_specs=P(None, blk, grp),
        check_vma=False,
    )
```

```python
import math

import jax
import jax.numpy as jnp
from jax import lax
from jax.experimental import pallas as pl
from jax.experimental.pallas import tpu as pltpu
from jax.sharding import Mesh
from jax.sharding import PartitionSpec as P

MESH = pl.DeviceIdType.MESH
NAMES = ("y", "zl", "core", "zh", "x")
Y, ZL, CORES, ZH, X = 4, 4, 2, 2, 4
GROUP = ZH * X
SUBS, ROWS, D, ROUNDS, PAIRS, MEMBERS = 4, 32, 256, 2, 16, 128
DRAWS = GROUP * ROWS
HALF = SUBS // 2
SLOTS = 8
PIECES = 2
LOG2E = math.log2(math.e)
LN2 = math.log(2.0)
NT = (((1,), (1,)), ((), ()))


def split(value):
    high = value.astype(jnp.bfloat16)
    low = (value - high.astype(jnp.float32)).astype(jnp.bfloat16)
    return high, low


def nt_dot(a, b):
    return lax.dot_general(a, b, NT, preferred_element_type=jnp.float32)


def row_sums(value):
    ones = jnp.ones((8, value.shape[1]), jnp.bfloat16)
    high, low = split(value)
    lowest = (value - high.astype(jnp.float32) - low.astype(jnp.float32)).astype(jnp.bfloat16)
    return (nt_dot(ones, high) + nt_dot(ones, low) + nt_dot(ones, lowest))[0:1]


def log_sum(pieces):
    peak = jnp.max(pieces, 0)
    return peak + jnp.log2(jnp.sum(jnp.exp2(pieces - peak[None]), 0))


def kernel(
    table_hbm, picks_hbm, bands_hbm, own, out,
    table, picks, bands,
    keys, queries, parts_hi, parts_lo, query_half, sums_out, sums_in, pair_out, pair_in,
    pick_out, pick_in, final_out, final_in, local_sem,
    z_send, z_recv, y_send, y_recv, half_send, half_recv, sib_send, sib_recv,
    r_send, r_recv, x_send, x_recv, xhalf_send, xhalf_recv,
    p_send, p_recv, l_send, l_recv, pair_send, pair_recv, f_send, f_recv,
):
    y, zl, core, zh, x = (lax.axis_index(name) for name in NAMES)
    me = zh * X + x

    def block(row, seg):
        return (row * ZL + seg) * CORES + core

    def copy(src, dst, send, recv, **where):
        return pltpu.make_async_remote_copy(
            src_ref=src, dst_ref=dst, send_sem=send, recv_sem=recv, device_id=where, device_id_type=MESH
        )

    y_up, y_down, y_far = (lax.rem(y + k, Y) for k in (1, 3, 2))
    x_up, x_down, x_far = (lax.rem(x + k, X) for k in (1, 3, 2))

    bottom, top = zl == 0, zl == ZL - 1
    z_up = {"zl": lax.rem(zl + 1, ZL), "zh": jnp.where(top, 1 - zh, zh)}
    z_down = {"zl": lax.rem(zl + ZL - 1, ZL), "zh": jnp.where(bottom, 1 - zh, zh)}
    barrier = pltpu.get_barrier_semaphore()
    greeted = [{"core": 1 - core}, z_up, z_down]
    greeted += [{"y": k} for k in (y_up, y_down)]
    greeted += [{"x": k} for k in (x_up, x_down)]
    for where in greeted:
        pl.semaphore_signal(barrier, inc=1, device_id=where, device_id_type=MESH)

    mine = block(y, zl)
    local = [
        pltpu.make_async_copy(src, dst, local_sem.at[n])
        for n, (src, dst) in enumerate(
            ((picks_hbm, picks), (own, keys.at[mine]), (own, queries.at[me]), (table_hbm, table), (bands_hbm, bands))
        )
    ]
    for made in local:
        made.start()

    sends = []

    def go(made):
        made.start()
        sends.append(made)
        return made

    low = zl < 2
    segs = [zl, zl + 1 - 2 * lax.rem(zl, 2), jnp.where(low, 2, 1), jnp.where(low, 3, 0)]
    y_copies, half_copies, sib_copies = {}, {}, []

    def piece(b, c, side=None):
        each = SUBS // PIECES
        if side is None:
            return b, pl.ds(c * each, each)
        if each > 1:
            return b, pl.ds(c * each + side * (each // 2), each // 2)
        return b, c, pl.ds(side * (ROWS // 2), ROWS // 2)

    def to_sibling(*where):
        n = len(sib_copies)
        part = keys.at[where]
        sib_copies.append(go(copy(part, part, sib_send.at[n], sib_recv.at[n], core=1 - core)))

    def z_copy(seg, c, up, fresh=False):
        where = piece(block(y, seg), c)
        return copy(
            own.at[where[1:]] if fresh else keys.at[where], keys.at[where],
            z_send.at[seg, c, int(up)], z_recv.at[seg, c], zl=zl + 1 if up else zl - 1,
        )

    def relay(seg, far, up, fresh=False, crossing=False):
        c = 0 if up else 1
        there = piece(block(Y, seg), c)
        here = piece(block(y, seg), c) if crossing else there
        return copy(
            own.at[here[1:]] if fresh else keys.at[here], keys.at[there],
            r_send.at[far, c], r_recv.at[far, c], **(z_up if up else z_down),
        )

    def along_y(k, c):
        where = piece(block(y, segs[k]), c)
        for side, to in enumerate((y_up, y_down)):
            y_copies[k, c, side] = go(
                copy(
                    own.at[where[1:]] if k == 0 else keys.at[where], keys.at[where], y_send.at[k, c, side], y_recv.at[k, c, side], y=to
                )
            )
        if k:
            to_sibling(*where)

    def along_y_again(k, c):
        for side, (origin, to) in enumerate(((y_down, y_up), (y_up, y_down))):
            b = block(origin, segs[k])
            y_copies[k, c, side].wait_recv()
            part = keys.at[piece(b, c, side)]
            half_copies[k, c, side] = go(
                copy(part, part, half_send.at[k, c, side], half_recv.at[k, c, side], y=to)
            )
            to_sibling(*piece(b, c))

    def far_arrived(k, c):
        for side in range(2):
            half_copies[k, c, side].wait_recv()
        to_sibling(*piece(block(y_far, segs[k]), c))

    def z_onward(k, c, act):
        seg, fresh = segs[k], k == 0

        @pl.when((seg <= zl) & ~top)
        def _():
            act(z_copy(seg, c, True, fresh))

        @pl.when((seg >= zl) & ~bottom)
        def _():
            act(z_copy(seg, c, False, fresh))

        if c == 0:

            @pl.when((seg <= zl) & top)
            def _():
                act(relay(seg, zl - seg, True, fresh, True))

        if c == PIECES - 1:

            @pl.when((seg >= zl) & bottom)
            def _():
                act(relay(seg, seg - zl, False, fresh, True))

    def z_arrived(k, c):
        z_copy(segs[k], c, True).wait_recv()
        z_onward(k, c, lambda made: made.start())

    def relay_onward(n, act, arrived):
        for up in (True, False):
            seg = lax.rem(zl + ZL - n, ZL) if up else lax.rem(zl + n, ZL)

            @pl.when(zl < n if up else ZL - 1 - zl < n)
            def _():
                if arrived:
                    relay(seg, n - 1, up).wait_recv()
                if n < ZL:
                    act(relay(seg, n, up))

    def relayed(n):
        relay_onward(n, lambda made: made.start(), True)

    x_copies, xhalf_copies = {}, {}

    def along_x(k):
        slot = lax.rem(zh + k, ZH) * X + x
        for side, to in enumerate((x_up, x_down)):
            x_copies[k, side] = go(
                copy(
                    queries.at[slot] if k else own, queries.at[slot],
                    x_send.at[k, side], x_recv.at[k, side], x=to,
                )
            )

    def along_x_again(k):
        for side, (origin, to) in enumerate(((x_down, x_up), (x_up, x_down))):
            slot = lax.rem(zh + k, ZH) * X + origin
            x_copies[k, side].wait_recv()
            part = queries.at[slot, pl.ds(side * HALF, HALF)]
            xhalf_copies[k, side] = go(copy(part, part, xhalf_send.at[k, side], xhalf_recv.at[k, side], x=to))

    def prepare(k):
        for side in range(2):
            xhalf_copies[k, side].wait_recv()
        half = lax.rem(zh + k, ZH)
        these = pl.ds(pl.multiple_of(half * X * ROWS, X * ROWS), X * ROWS)
        for m in range(SUBS):
            rows = queries[pl.ds(half * X, X), m].reshape(X * ROWS, D)
            high, low = split(rows)
            parts_hi[m, these] = high
            parts_lo[m, these] = low
            query_half[m, :, these] = jnp.broadcast_to(0.5 * row_sums(rows * rows), (8, X * ROWS))

    axes = [
        [{"core": 1 - core}],
        [{"zl": lax.rem(zl + k, ZL)} for k in range(1, ZL)],
        [{"y": lax.rem(y + k, Y)} for k in range(1, Y)],
        [{"x": lax.rem(x + k, X)} for k in range(1, X)],
        [{"zh": 1 - zh}],
    ]
    pick_copies = {}

    def picks_along(a):
        for n, where in enumerate(axes[a]):
            pick_copies[a, n] = go(
                copy(pick_out.at[a], pick_in.at[a, n], p_send.at[a, n], p_recv.at[a, n], **where)
            )

    def picks_arrived(a):
        total = pick_out[a]
        for n in range(len(axes[a])):
            pick_copies[a, n].wait_recv()
            total += pick_in[a, n]
        pick_out[a + 1] = total

    every = range(PIECES)
    pl.semaphore_wait(barrier, len(greeted))
    for c in every:
        z_onward(0, c, lambda made: made.start())
        along_y(0, c)
    along_x(0)

    for made in local[:3]:
        made.wait()
    to_sibling(mine)
    number = lax.broadcasted_iota(jnp.int32, (ROWS, D), 0)
    pick_out[0] = jnp.zeros((8, 128), jnp.float32)
    for t in range(ROUNDS):
        total = jnp.zeros((ROWS, D), jnp.float32)
        for m in range(SUBS):
            total += jnp.where(number == picks[t, m] - me * ROWS, queries[me, m], 0.0)
        total = jnp.sum(total, 0, keepdims=True)
        for side in range(2):
            pick_out[0, 2 * t + side : 2 * t + side + 1] = total[:, 128 * side : 128 * side + 128]
    picks_along(0)

    for c in every:
        z_arrived(1, c)
        along_y(1, c)
    relayed(1)
    for c in every:
        along_y_again(0, c)
    along_x_again(0)
    for c in every:
        z_arrived(2, c)
        along_y(2, c)
    relayed(2)
    for c in every:
        along_y_again(1, c)
    for c in every:
        z_arrived(3, c)
        along_y(3, c)
    relayed(3)
    for c in every:
        far_arrived(0, c)
    for c in every:
        along_y_again(2, c)
    picks_arrived(0)
    picks_along(1)
    prepare(0)
    relayed(4)
    queries[(1 - zh) * X + x] = keys[block(Y, zl)]
    along_x(1)
    picks_arrived(1)
    picks_along(2)
    for c in every:
        far_arrived(1, c)
    picks_arrived(2)
    picks_along(3)
    for c in every:
        along_y_again(3, c)
    along_x_again(1)
    for c in every:
        far_arrived(2, c)
    picks_arrived(3)
    picks_along(4)
    prepare(1)

    for made in local[3:]:
        made.wait()

    band = []
    for t in range(ROUNDS):
        index = jnp.full((1, DRAWS), bands[t], jnp.int32).astype(jnp.float32)
        band.append((D / 32.0) * (1.0 + index / 256.0))
    for c in every:
        far_arrived(3, c)
    for made in sib_copies:
        made.wait_recv()

    l_copies = []
    for n, m in enumerate((x_far, x_up, x_down, x)):
        high, low = parts_hi[m], parts_lo[m]
        shift = query_half[m, 0:1]
        for first in range(0, PAIRS, SLOTS):
            rows = []
            for s in range(first, first + SLOTS):
                p = table[m, s]
                rows.append(keys[lax.div(p, SUBS), lax.rem(p, SUBS)])
            rows = jnp.concatenate(rows, 0)
            norm_half = 0.5 * jnp.sum(rows * rows, -1, keepdims=True)
            key_high, key_low = split(rows)
            product = nt_dot(key_high, high) + nt_dot(key_low, high) + nt_dot(key_high, low)
            value = (product - norm_half).reshape(SLOTS, ROWS, DRAWS)
            peak = jnp.max(value, 1, keepdims=True)
            value = value - peak
            peak = peak.reshape(SLOTS, DRAWS) - shift
            for t in range(ROUNDS):
                rate = LOG2E / band[t]
                mass = jnp.sum(jnp.exp2(value * rate[None]), 1)
                sums_out[m, t, pl.ds(first, SLOTS)] = peak * rate + jnp.log2(mass)
        if n < X - 1:
            l_copies.append(go(copy(sums_out.at[m], sums_in.at[n], l_send.at[n], l_recv.at[n], x=m)))
        else:
            sums_in[n] = sums_out[m]

    for made in l_copies:
        made.wait_recv()
    pair_out[...] = log_sum(sums_in[...])
    pair_copy = go(copy(pair_out, pair_in, pair_send, pair_recv, zh=1 - zh))
    spread = []
    picks_arrived(4)
    for t in range(ROUNDS):
        centre = jnp.concatenate([pick_out[5, 2 * t : 2 * t + 1], pick_out[5, 2 * t + 1 : 2 * t + 2]], 1)
        away = queries[:, x].reshape(DRAWS, D) - centre / MEMBERS
        spread.append(row_sums(away * away) / (2.0 * band[t]))
    pair_copy.wait_recv()
    first, second = pair_out[...], pair_in[...]
    peak = jnp.maximum(first, second)
    whole = peak + jnp.log2(jnp.exp2(first - peak) + jnp.exp2(second - peak))
    for t in range(ROUNDS):
        logits = (LN2 / PAIRS) * jnp.sum(whole[t], 0, keepdims=True) - spread[t]
        logits = logits - jnp.max(logits, -1, keepdims=True)
        result = logits - jnp.log(jnp.sum(jnp.exp(logits), -1, keepdims=True))
        result = jnp.where(zh == 0, result[:, : X * ROWS], result[:, X * ROWS :])
        for k in range(X):
            final_out[k, t : t + 1, 0:ROWS] = result[:, k * ROWS : (k + 1) * ROWS]
    f_copies = []
    for n, k in enumerate((x_far, x_up, x_down)):
        f_copies.append(go(copy(final_out.at[k], final_in.at[x], f_send.at[n], f_recv.at[n], x=k)))
    final_in[x] = final_out[x]
    for made in f_copies:
        made.wait_recv()
    for m in range(SUBS):
        out[:, m] = final_in[m, 0:ROUNDS, 0:ROWS]
    for made in sends:
        made.wait_send()
    for k in range(ZL):
        for c in every:
            z_onward(k, c, lambda made: made.wait_send())
        if k:
            relay_onward(k, lambda made: made.wait_send(), False)


def per_device(samples, pair_table, assignment, band_index):
    dma = pltpu.SemaphoreType.DMA
    hbm = pl.BlockSpec(memory_space=pltpu.HBM)
    vmem = pl.BlockSpec(memory_space=pltpu.VMEM)
    f32 = jnp.float32
    siblings = 1 + (Y * ZL - 1) * PIECES
    return pl.pallas_call(
        kernel,
        name="weights",
        out_shape=jax.ShapeDtypeStruct((ROUNDS, SUBS, ROWS), f32),
        in_specs=[hbm] * 4,
        out_specs=vmem,
        scratch_shapes=[
            pltpu.SMEM((SUBS, PAIRS), jnp.int32),
            pltpu.SMEM((ROUNDS, SUBS), jnp.int32),
            pltpu.SMEM((ROUNDS,), jnp.int32),
            pltpu.VMEM(((Y + 1) * ZL * CORES, SUBS, ROWS, D), f32),
            pltpu.VMEM((GROUP, SUBS, ROWS, D), f32),
            pltpu.VMEM((SUBS, DRAWS, D), jnp.bfloat16),
            pltpu.VMEM((SUBS, DRAWS, D), jnp.bfloat16),
            pltpu.VMEM((SUBS, 8, DRAWS), f32),
            pltpu.VMEM((SUBS, ROUNDS, PAIRS, DRAWS), f32),
            pltpu.VMEM((X, ROUNDS, PAIRS, DRAWS), f32),
            pltpu.VMEM((ROUNDS, PAIRS, DRAWS), f32),
            pltpu.VMEM((ROUNDS, PAIRS, DRAWS), f32),
            pltpu.VMEM((6, 8, 128), f32),
            pltpu.VMEM((5, 3, 8, 128), f32),
            pltpu.VMEM((X, 8, 128), f32),
            pltpu.VMEM((X, 8, 128), f32),
            dma((5,)),
            dma((ZL, PIECES, 2)), dma((ZL, PIECES)),
            dma((ZL, PIECES, 2)), dma((ZL, PIECES, 2)),
            dma((ZL, PIECES, 2)), dma((ZL, PIECES, 2)),
            dma((siblings,)), dma((siblings,)),
            dma((ZL, 2)), dma((ZL, 2)),
            dma((ZH, 2)), dma((ZH, 2)),
            dma((ZH, 2)), dma((ZH, 2)),
            dma((5, 3)), dma((5, 3)),
            dma((X - 1,)), dma((X - 1,)),
            dma, dma,
            dma((X - 1,)), dma((X - 1,)),
        ],
        compiler_params=pltpu.CompilerParams(
            collective_id=0, has_side_effects=True, vmem_limit_bytes=60 * 1024 * 1024
        ),
    )(pair_table, assignment, band_index, samples)


def solution(mesh):
    finer = Mesh(mesh.devices.reshape(Y, ZL, CORES, ZH, X), NAMES)
    blk, grp = NAMES[:3], NAMES[3:]
    return jax.shard_map(
        per_device,
        mesh=finer,
        in_specs=(P(blk, grp, None), P(blk, None), P(None, blk), P()),
        out_specs=P(None, blk, grp),
        check_vma=False,
    )
```

```python
import math

import jax
import jax.numpy as jnp
from jax import lax
from jax.experimental import pallas as pl
from jax.experimental.pallas import tpu as pltpu
from jax.sharding import Mesh
from jax.sharding import PartitionSpec as P

MESH = pl.DeviceIdType.MESH
NAMES = ("y", "zl", "core", "zh", "x")
Y, ZL, CORES, ZH, X = 4, 4, 2, 2, 4
GROUP = ZH * X
SUBS, ROWS, D, ROUNDS, PAIRS, MEMBERS = 4, 32, 256, 2, 16, 128
DRAWS = GROUP * ROWS
HALF = SUBS // 2
SLOTS = 8
PIECES = 2
LOG2E = math.log2(math.e)
LN2 = math.log(2.0)
NT = (((1,), (1,)), ((), ()))


def split(value):
    high = value.astype(jnp.bfloat16)
    low = (value - high.astype(jnp.float32)).astype(jnp.bfloat16)
    return high, low


def nt_dot(a, b):
    return lax.dot_general(a, b, NT, preferred_element_type=jnp.float32)


def row_sums(value):
    ones = jnp.ones((8, value.shape[1]), jnp.bfloat16)
    high, low = split(value)
    lowest = (value - high.astype(jnp.float32) - low.astype(jnp.float32)).astype(jnp.bfloat16)
    return (nt_dot(ones, high) + nt_dot(ones, low) + nt_dot(ones, lowest))[0:1]


def log_sum(pieces):
    peak = jnp.max(pieces, 0)
    return peak + jnp.log2(jnp.sum(jnp.exp2(pieces - peak[None]), 0))


def kernel(
    table_hbm, picks_hbm, bands_hbm, own, out,
    table, picks, bands,
    keys, queries, parts, query_half, sums_out, sums_in, pair_out, pair_in,
    pick_out, pick_in, final_out, final_in, local_sem,
    z_send, z_recv, y_send, y_recv, half_send, half_recv, sib_send, sib_recv,
    r_send, r_recv, x_send, x_recv,
    p_send, p_recv, l_send, l_recv, pair_send, pair_recv, f_send, f_recv,
):
    y, zl, core, zh, x = (lax.axis_index(name) for name in NAMES)
    me = zh * X + x

    def block(row, seg):
        return (row * ZL + seg) * CORES + core

    def copy(src, dst, send, recv, **where):
        return pltpu.make_async_remote_copy(
            src_ref=src, dst_ref=dst, send_sem=send, recv_sem=recv, device_id=where, device_id_type=MESH
        )

    y_up, y_down, y_far = (lax.rem(y + k, Y) for k in (1, 3, 2))
    x_up, x_down, x_far = (lax.rem(x + k, X) for k in (1, 3, 2))

    bottom, top = zl == 0, zl == ZL - 1
    z_up = {"zl": lax.rem(zl + 1, ZL), "zh": jnp.where(top, 1 - zh, zh)}
    z_down = {"zl": lax.rem(zl + ZL - 1, ZL), "zh": jnp.where(bottom, 1 - zh, zh)}
    barrier = pltpu.get_barrier_semaphore()
    greeted = [{"core": 1 - core}, z_up, z_down]
    greeted += [{"y": k} for k in (y_up, y_down)]
    greeted += [{"x": k} for k in (x_up, x_down, x_far)]
    for where in greeted:
        pl.semaphore_signal(barrier, inc=1, device_id=where, device_id_type=MESH)

    mine = block(y, zl)
    local = [
        pltpu.make_async_copy(src, dst, local_sem.at[n])
        for n, (src, dst) in enumerate(
            ((picks_hbm, picks), (own, keys.at[mine]), (own, queries.at[me]), (table_hbm, table), (bands_hbm, bands))
        )
    ]
    for made in local:
        made.start()

    sends = []

    def go(made):
        made.start()
        sends.append(made)
        return made

    low = zl < 2
    segs = [zl, zl + 1 - 2 * lax.rem(zl, 2), jnp.where(low, 2, 1), jnp.where(low, 3, 0)]
    y_copies, half_copies, sib_copies = {}, {}, []

    def piece(b, c, side=None):
        each = SUBS // PIECES
        if side is None:
            return b, pl.ds(c * each, each)
        if each > 1:
            return b, pl.ds(c * each + side * (each // 2), each // 2)
        return b, c, pl.ds(side * (ROWS // 2), ROWS // 2)

    def to_sibling(*where):
        n = len(sib_copies)
        part = keys.at[where]
        sib_copies.append(go(copy(part, part, sib_send.at[n], sib_recv.at[n], core=1 - core)))

    def z_copy(seg, c, up, fresh=False):
        where = piece(block(y, seg), c)
        return copy(
            own.at[where[1:]] if fresh else keys.at[where], keys.at[where],
            z_send.at[seg, c, int(up)], z_recv.at[seg, c], zl=zl + 1 if up else zl - 1,
        )

    def relay(seg, far, up, fresh=False, crossing=False):
        c = 0 if up else 1
        there = piece(block(Y, seg), c)
        here = piece(block(y, seg), c) if crossing else there
        return copy(
            own.at[here[1:]] if fresh else keys.at[here], keys.at[there],
            r_send.at[far, c], r_recv.at[far, c], **(z_up if up else z_down),
        )

    def along_y(k, c):
        where = piece(block(y, segs[k]), c)
        for side, to in enumerate((y_up, y_down)):
            y_copies[k, c, side] = go(
                copy(
                    own.at[where[1:]] if k == 0 else keys.at[where], keys.at[where], y_send.at[k, c, side], y_recv.at[k, c, side], y=to
                )
            )
        if k:
            to_sibling(*where)

    def along_y_again(k, c):
        for side, (origin, to) in enumerate(((y_down, y_up), (y_up, y_down))):
            b = block(origin, segs[k])
            y_copies[k, c, side].wait_recv()
            part = keys.at[piece(b, c, side)]
            half_copies[k, c, side] = go(
                copy(part, part, half_send.at[k, c, side], half_recv.at[k, c, side], y=to)
            )
            to_sibling(*piece(b, c))

    def far_arrived(k, c):
        for side in range(2):
            half_copies[k, c, side].wait_recv()
        to_sibling(*piece(block(y_far, segs[k]), c))

    def z_onward(k, c, act):
        seg, fresh = segs[k], k == 0

        @pl.when((seg <= zl) & ~top)
        def _():
            act(z_copy(seg, c, True, fresh))

        @pl.when((seg >= zl) & ~bottom)
        def _():
            act(z_copy(seg, c, False, fresh))

        if c == 0:

            @pl.when((seg <= zl) & top)
            def _():
                act(relay(seg, zl - seg, True, fresh, True))

        if c == PIECES - 1:

            @pl.when((seg >= zl) & bottom)
            def _():
                act(relay(seg, seg - zl, False, fresh, True))

    def z_arrived(k, c):
        z_copy(segs[k], c, True).wait_recv()
        z_onward(k, c, lambda made: made.start())

    def relay_onward(n, act, arrived):
        for up in (True, False):
            seg = lax.rem(zl + ZL - n, ZL) if up else lax.rem(zl + n, ZL)

            @pl.when(zl < n if up else ZL - 1 - zl < n)
            def _():
                if arrived:
                    relay(seg, n - 1, up).wait_recv()
                if n < ZL:
                    act(relay(seg, n, up))

    def relayed(n):
        relay_onward(n, lambda made: made.start(), True)

    x_copies = {}

    def along_x(k, c):
        where = piece(lax.rem(zh + k, ZH) * X + x, c)
        for n, to in enumerate((x_far, x_up, x_down)):
            x_copies[k, c, n] = go(
                copy(
                    queries.at[where] if k else own.at[where[1:]], queries.at[where],
                    x_send.at[k, c, n], x_recv.at[k, c, n], x=to,
                )
            )

    def prepare(k):
        for c in range(PIECES):
            for n in range(X - 1):
                x_copies[k, c, n].wait_recv()
        half = lax.rem(zh + k, ZH)
        these = pl.ds(pl.multiple_of(half * X * ROWS, X * ROWS), X * ROWS)
        for m in range(SUBS):
            rows = queries[pl.ds(half * X, X), m].reshape(X * ROWS, D)
            high, low = split(rows)
            parts[m, these] = jnp.concatenate([high, high, low], 1)
            query_half[m, :, these] = jnp.broadcast_to(0.5 * row_sums(rows * rows), (8, X * ROWS))

    axes = [
        [{"core": 1 - core}],
        [{"zl": lax.rem(zl + k, ZL)} for k in range(1, ZL)],
        [{"y": lax.rem(y + k, Y)} for k in range(1, Y)],
        [{"x": lax.rem(x + k, X)} for k in range(1, X)],
        [{"zh": 1 - zh}],
    ]
    pick_copies = {}

    def picks_along(a):
        for n, where in enumerate(axes[a]):
            pick_copies[a, n] = go(
                copy(pick_out.at[a], pick_in.at[a, n], p_send.at[a, n], p_recv.at[a, n], **where)
            )

    def picks_arrived(a):
        total = pick_out[a]
        for n in range(len(axes[a])):
            pick_copies[a, n].wait_recv()
            total += pick_in[a, n]
        pick_out[a + 1] = total

    every = range(PIECES)
    pl.semaphore_wait(barrier, len(greeted))
    for c in every:
        z_onward(0, c, lambda made: made.start())
        along_y(0, c)
    for c in every:
        along_x(0, c)

    for made in local[:3]:
        made.wait()
    to_sibling(mine)
    number = lax.broadcasted_iota(jnp.int32, (ROWS, D), 0)
    pick_out[0] = jnp.zeros((8, 128), jnp.float32)
    for t in range(ROUNDS):
        total = jnp.zeros((ROWS, D), jnp.float32)
        for m in range(SUBS):
            total += jnp.where(number == picks[t, m] - me * ROWS, queries[me, m], 0.0)
        total = jnp.sum(total, 0, keepdims=True)
        for side in range(2):
            pick_out[0, 2 * t + side : 2 * t + side + 1] = total[:, 128 * side : 128 * side + 128]
    picks_along(0)

    for c in every:
        z_arrived(1, c)
        along_y(1, c)
    relayed(1)
    for c in every:
        along_y_again(0, c)
    for c in every:
        z_arrived(2, c)
        along_y(2, c)
    relayed(2)
    for c in every:
        along_y_again(1, c)
    for c in every:
        z_arrived(3, c)
        along_y(3, c)
    relayed(3)
    picks_arrived(0)
    picks_along(1)
    for c in every:
        far_arrived(0, c)
    for c in every:
        along_y_again(2, c)
    picks_arrived(1)
    picks_along(2)
    prepare(0)
    relayed(4)
    queries[(1 - zh) * X + x] = keys[block(Y, zl)]
    for c in every:
        along_x(1, c)
    for c in every:
        far_arrived(1, c)
    picks_arrived(2)
    picks_along(3)
    for c in every:
        along_y_again(3, c)
    for c in every:
        far_arrived(2, c)
    prepare(1)

    for made in local[3:]:
        made.wait()

    band = []
    for t in range(ROUNDS):
        index = jnp.full((1, DRAWS), bands[t], jnp.int32).astype(jnp.float32)
        band.append((D / 32.0) * (1.0 + index / 256.0))
    for c in every:
        far_arrived(3, c)
    for made in sib_copies:
        made.wait_recv()

    picks_arrived(3)
    picks_along(4)
    l_copies = []
    for n, m in enumerate((x_far, x_up, x_down, x)):
        shift = query_half[m, 0:1]
        for first in range(0, PAIRS, SLOTS):
            rows = []
            for s in range(first, first + SLOTS):
                p = table[m, s]
                rows.append(keys[lax.div(p, SUBS), lax.rem(p, SUBS)])
            rows = jnp.concatenate(rows, 0)
            norm_half = 0.5 * jnp.sum(rows * rows, -1, keepdims=True)
            key_high, key_low = split(rows)
            product = nt_dot(jnp.concatenate([key_high, key_low, key_high], 1), parts[m])
            value = (product - norm_half).reshape(SLOTS, ROWS, DRAWS)
            peak = jnp.max(value, 1, keepdims=True)
            value = value - peak
            peak = peak.reshape(SLOTS, DRAWS) - shift
            for t in range(ROUNDS):
                rate = LOG2E / band[t]
                mass = jnp.sum(jnp.exp2(value * rate[None]), 1)
                sums_out[m, t, pl.ds(first, SLOTS)] = peak * rate + jnp.log2(mass)
        if n < X - 1:
            l_copies.append(go(copy(sums_out.at[m], sums_in.at[n], l_send.at[n], l_recv.at[n], x=m)))
        else:
            sums_in[n] = sums_out[m]

    for made in l_copies:
        made.wait_recv()
    pair_out[...] = log_sum(sums_in[...])
    pair_copy = go(copy(pair_out, pair_in, pair_send, pair_recv, zh=1 - zh))
    spread = []
    picks_arrived(4)
    for t in range(ROUNDS):
        centre = jnp.concatenate([pick_out[5, 2 * t : 2 * t + 1], pick_out[5, 2 * t + 1 : 2 * t + 2]], 1)
        away = queries[:, x].reshape(DRAWS, D) - centre / MEMBERS
        spread.append(row_sums(away * away) / (2.0 * band[t]))
    while sends[0] is not pair_copy:
        sends.pop(0).wait_send()
    for k in range(ZL):
        for c in every:
            z_onward(k, c, lambda made: made.wait_send())
        if k:
            relay_onward(k, lambda made: made.wait_send(), False)
    pair_copy.wait_recv()
    first, second = pair_out[...], pair_in[...]
    peak = jnp.maximum(first, second)
    whole = peak + jnp.log2(jnp.exp2(first - peak) + jnp.exp2(second - peak))
    for t in range(ROUNDS):
        logits = (LN2 / PAIRS) * jnp.sum(whole[t], 0, keepdims=True) - spread[t]
        logits = logits - jnp.max(logits, -1, keepdims=True)
        result = logits - jnp.log(jnp.sum(jnp.exp(logits), -1, keepdims=True))
        result = jnp.where(zh == 0, result[:, : X * ROWS], result[:, X * ROWS :])
        for k in range(X):
            final_out[k, t : t + 1, 0:ROWS] = result[:, k * ROWS : (k + 1) * ROWS]
    f_copies = []
    for n, k in enumerate((x_far, x_up, x_down)):
        f_copies.append(go(copy(final_out.at[k], final_in.at[x], f_send.at[n], f_recv.at[n], x=k)))
    final_in[x] = final_out[x]
    for made in f_copies:
        made.wait_recv()
    for m in range(SUBS):
        out[:, m] = final_in[m, 0:ROUNDS, 0:ROWS]
    for made in sends:
        made.wait_send()


def per_device(samples, pair_table, assignment, band_index):
    dma = pltpu.SemaphoreType.DMA
    hbm = pl.BlockSpec(memory_space=pltpu.HBM)
    vmem = pl.BlockSpec(memory_space=pltpu.VMEM)
    f32 = jnp.float32
    siblings = 1 + (Y * ZL - 1) * PIECES
    return pl.pallas_call(
        kernel,
        name="weights",
        out_shape=jax.ShapeDtypeStruct((ROUNDS, SUBS, ROWS), f32),
        in_specs=[hbm] * 4,
        out_specs=vmem,
        scratch_shapes=[
            pltpu.SMEM((SUBS, PAIRS), jnp.int32),
            pltpu.SMEM((ROUNDS, SUBS), jnp.int32),
            pltpu.SMEM((ROUNDS,), jnp.int32),
            pltpu.VMEM(((Y + 1) * ZL * CORES, SUBS, ROWS, D), f32),
            pltpu.VMEM((GROUP, SUBS, ROWS, D), f32),
            pltpu.VMEM((SUBS, DRAWS, 3 * D), jnp.bfloat16),
            pltpu.VMEM((SUBS, 8, DRAWS), f32),
            pltpu.VMEM((SUBS, ROUNDS, PAIRS, DRAWS), f32),
            pltpu.VMEM((X, ROUNDS, PAIRS, DRAWS), f32),
            pltpu.VMEM((ROUNDS, PAIRS, DRAWS), f32),
            pltpu.VMEM((ROUNDS, PAIRS, DRAWS), f32),
            pltpu.VMEM((6, 8, 128), f32),
            pltpu.VMEM((5, 3, 8, 128), f32),
            pltpu.VMEM((X, 8, 128), f32),
            pltpu.VMEM((X, 8, 128), f32),
            dma((5,)),
            dma((ZL, PIECES, 2)), dma((ZL, PIECES)),
            dma((ZL, PIECES, 2)), dma((ZL, PIECES, 2)),
            dma((ZL, PIECES, 2)), dma((ZL, PIECES, 2)),
            dma((siblings,)), dma((siblings,)),
            dma((ZL, 2)), dma((ZL, 2)),
            dma((ZH, PIECES, X - 1)), dma((ZH, PIECES, X - 1)),
            dma((5, 3)), dma((5, 3)),
            dma((X - 1,)), dma((X - 1,)),
            dma, dma,
            dma((X - 1,)), dma((X - 1,)),
        ],
        compiler_params=pltpu.CompilerParams(
            collective_id=0, has_side_effects=True, vmem_limit_bytes=60 * 1024 * 1024
        ),
    )(pair_table, assignment, band_index, samples)


def solution(mesh):
    finer = Mesh(mesh.devices.reshape(Y, ZL, CORES, ZH, X), NAMES)
    blk, grp = NAMES[:3], NAMES[3:]
    return jax.shard_map(
        per_device,
        mesh=finer,
        in_specs=(P(blk, grp, None), P(blk, None), P(None, blk), P()),
        out_specs=P(None, blk, grp),
        check_vma=False,
    )
```

```python
import math

import jax
import jax.numpy as jnp
from jax import lax
from jax.experimental import pallas as pl
from jax.experimental.pallas import tpu as pltpu
from jax.sharding import Mesh
from jax.sharding import PartitionSpec as P

MESH = pl.DeviceIdType.MESH
NAMES = ("y", "zl", "core", "zh", "x")
Y, ZL, CORES, ZH, X = 4, 4, 2, 2, 4
GROUP = ZH * X
SUBS, ROWS, D, ROUNDS, PAIRS, MEMBERS = 4, 32, 256, 2, 16, 128
DRAWS = GROUP * ROWS
HALF = SUBS // 2
SLOTS = 8
PIECES = 2
LOG2E = math.log2(math.e)
LN2 = math.log(2.0)
NT = (((1,), (1,)), ((), ()))


def split(value):
    high = value.astype(jnp.bfloat16)
    low = (value - high.astype(jnp.float32)).astype(jnp.bfloat16)
    return high, low


def nt_dot(a, b):
    return lax.dot_general(a, b, NT, preferred_element_type=jnp.float32)


def row_sums(value):
    ones = jnp.ones((8, value.shape[1]), jnp.bfloat16)
    high, low = split(value)
    lowest = (value - high.astype(jnp.float32) - low.astype(jnp.float32)).astype(jnp.bfloat16)
    return (nt_dot(ones, high) + nt_dot(ones, low) + nt_dot(ones, lowest))[0:1]


def log_sum(pieces):
    peak = jnp.max(pieces, 0)
    return peak + jnp.log2(jnp.sum(jnp.exp2(pieces - peak[None]), 0))


def kernel(
    table_hbm, picks_hbm, bands_hbm, own, out,
    table, picks, bands,
    keys, queries, parts, query_half, sums_out, sums_in, pair_out, pair_in,
    pick_out, pick_in, final_out, final_in, local_sem,
    z_send, z_recv, y_send, y_recv, half_send, half_recv, sib_send, sib_recv,
    r_send, r_recv, x_send, x_recv,
    p_send, p_recv, l_send, l_recv, pair_send, pair_recv, f_send, f_recv,
):
    y, zl, core, zh, x = (lax.axis_index(name) for name in NAMES)
    me = zh * X + x

    def block(row, seg):
        return (row * ZL + seg) * CORES + core

    def copy(src, dst, send, recv, **where):
        return pltpu.make_async_remote_copy(
            src_ref=src, dst_ref=dst, send_sem=send, recv_sem=recv, device_id=where, device_id_type=MESH
        )

    y_up, y_down, y_far = (lax.rem(y + k, Y) for k in (1, 3, 2))
    x_up, x_down, x_far = (lax.rem(x + k, X) for k in (1, 3, 2))

    bottom, top = zl == 0, zl == ZL - 1
    z_up = {"zl": lax.rem(zl + 1, ZL), "zh": jnp.where(top, 1 - zh, zh)}
    z_down = {"zl": lax.rem(zl + ZL - 1, ZL), "zh": jnp.where(bottom, 1 - zh, zh)}
    barrier = pltpu.get_barrier_semaphore()
    greeted = [{"core": 1 - core}, z_up, z_down]
    greeted += [{"y": k} for k in (y_up, y_down)]
    greeted += [{"x": k} for k in (x_up, x_down, x_far)]
    for where in greeted:
        pl.semaphore_signal(barrier, inc=1, device_id=where, device_id_type=MESH)

    mine = block(y, zl)
    local = [
        pltpu.make_async_copy(src, dst, local_sem.at[n])
        for n, (src, dst) in enumerate(
            ((picks_hbm, picks), (own, keys.at[mine]), (own, queries.at[me]), (table_hbm, table), (bands_hbm, bands))
        )
    ]
    for made in local:
        made.start()

    sends = []

    def go(made):
        made.start()
        sends.append(made)
        return made

    low = zl < 2
    segs = [zl, zl + 1 - 2 * lax.rem(zl, 2), jnp.where(low, 2, 1), jnp.where(low, 3, 0)]
    y_copies, half_copies, sib_copies = {}, {}, []

    def piece(b, c, side=None):
        each = SUBS // PIECES
        if side is None:
            return b, pl.ds(c * each, each)
        if each > 1:
            return b, pl.ds(c * each + side * (each // 2), each // 2)
        return b, c, pl.ds(side * (ROWS // 2), ROWS // 2)

    def to_sibling(*where):
        n = len(sib_copies)
        part = keys.at[where]
        sib_copies.append(go(copy(part, part, sib_send.at[n], sib_recv.at[n], core=1 - core)))

    def z_copy(seg, c, up, fresh=False):
        where = piece(block(y, seg), c)
        return copy(
            own.at[where[1:]] if fresh else keys.at[where], keys.at[where],
            z_send.at[seg, c, int(up)], z_recv.at[seg, c], zl=zl + 1 if up else zl - 1,
        )

    def relay(seg, far, up, fresh=False, crossing=False):
        c = 0 if up else 1
        there = piece(block(Y, seg), c)
        here = piece(block(y, seg), c) if crossing else there
        return copy(
            own.at[here[1:]] if fresh else keys.at[here], keys.at[there],
            r_send.at[far, c], r_recv.at[far, c], **(z_up if up else z_down),
        )

    def along_y(k, c):
        where = piece(block(y, segs[k]), c)
        for side, to in enumerate((y_up, y_down)):
            y_copies[k, c, side] = go(
                copy(
                    own.at[where[1:]] if k == 0 else keys.at[where], keys.at[where], y_send.at[k, c, side], y_recv.at[k, c, side], y=to
                )
            )
        if k:
            to_sibling(*where)

    def along_y_again(k, c):
        for side, (origin, to) in enumerate(((y_down, y_up), (y_up, y_down))):
            b = block(origin, segs[k])
            y_copies[k, c, side].wait_recv()
            part = keys.at[piece(b, c, side)]
            half_copies[k, c, side] = go(
                copy(part, part, half_send.at[k, c, side], half_recv.at[k, c, side], y=to)
            )
            to_sibling(*piece(b, c))

    def far_arrived(k, c):
        for side in range(2):
            half_copies[k, c, side].wait_recv()
        to_sibling(*piece(block(y_far, segs[k]), c))

    def z_onward(k, c, act):
        seg, fresh = segs[k], k == 0

        @pl.when((seg <= zl) & ~top)
        def _():
            act(z_copy(seg, c, True, fresh))

        @pl.when((seg >= zl) & ~bottom)
        def _():
            act(z_copy(seg, c, False, fresh))

        if c == 0:

            @pl.when((seg <= zl) & top)
            def _():
                act(relay(seg, zl - seg, True, fresh, True))

        if c == PIECES - 1:

            @pl.when((seg >= zl) & bottom)
            def _():
                act(relay(seg, seg - zl, False, fresh, True))

    def z_arrived(k, c):
        z_copy(segs[k], c, True).wait_recv()
        z_onward(k, c, lambda made: made.start())

    def relay_onward(n, act, arrived):
        for up in (True, False):
            seg = lax.rem(zl + ZL - n, ZL) if up else lax.rem(zl + n, ZL)

            @pl.when(zl < n if up else ZL - 1 - zl < n)
            def _():
                if arrived:
                    relay(seg, n - 1, up).wait_recv()
                if n < ZL:
                    act(relay(seg, n, up))

    def relayed(n):
        relay_onward(n, lambda made: made.start(), True)

    x_copies = {}

    def along_x(k, c):
        where = piece(lax.rem(zh + k, ZH) * X + x, c)
        for n, to in enumerate((x_far, x_up, x_down)):
            x_copies[k, c, n] = go(
                copy(
                    queries.at[where] if k else own.at[where[1:]], queries.at[where],
                    x_send.at[k, c, n], x_recv.at[k, c, n], x=to,
                )
            )

    def prepare(k):
        for c in range(PIECES):
            for n in range(X - 1):
                x_copies[k, c, n].wait_recv()
        half = lax.rem(zh + k, ZH)
        these = pl.ds(pl.multiple_of(half * X * ROWS, X * ROWS), X * ROWS)
        for m in range(SUBS):
            rows = queries[pl.ds(half * X, X), m].reshape(X * ROWS, D)
            high, low = split(rows)
            parts[m, these] = jnp.concatenate([high, high, low], 1)
            query_half[m, :, these] = jnp.broadcast_to(0.5 * row_sums(rows * rows), (8, X * ROWS))

    axes = [
        [{"core": 1 - core}],
        [{"zl": lax.rem(zl + k, ZL)} for k in range(1, ZL)],
        [{"y": lax.rem(y + k, Y)} for k in range(1, Y)],
        [{"x": lax.rem(x + k, X)} for k in range(1, X)],
        [{"zh": 1 - zh}],
    ]
    pick_copies = {}

    def picks_along(a):
        for n, where in enumerate(axes[a]):
            pick_copies[a, n] = go(
                copy(pick_out.at[a], pick_in.at[a, n], p_send.at[a, n], p_recv.at[a, n], **where)
            )

    def picks_arrived(a):
        total = pick_out[a]
        for n in range(len(axes[a])):
            pick_copies[a, n].wait_recv()
            total += pick_in[a, n]
        pick_out[a + 1] = total

    every = range(PIECES)
    pl.semaphore_wait(barrier, len(greeted))
    for c in every:
        z_onward(0, c, lambda made: made.start())
        along_y(0, c)
    for c in every:
        along_x(0, c)

    for made in local[:3]:
        made.wait()
    to_sibling(mine)
    number = lax.broadcasted_iota(jnp.int32, (ROWS, D), 0)
    pick_out[0] = jnp.zeros((8, 128), jnp.float32)
    for t in range(ROUNDS):
        total = jnp.zeros((ROWS, D), jnp.float32)
        for m in range(SUBS):
            total += jnp.where(number == picks[t, m] - me * ROWS, queries[me, m], 0.0)
        total = jnp.sum(total, 0, keepdims=True)
        for side in range(2):
            pick_out[0, 2 * t + side : 2 * t + side + 1] = total[:, 128 * side : 128 * side + 128]
    picks_along(0)

    for c in every:
        z_arrived(1, c)
        along_y(1, c)
    relayed(1)
    for c in every:
        z_arrived(2, c)
        along_y(2, c)
    for c in every:
        along_y_again(0, c)
    relayed(2)
    for c in every:
        along_y_again(1, c)
    for c in every:
        z_arrived(3, c)
        along_y(3, c)
    relayed(3)
    picks_arrived(0)
    picks_along(1)
    relayed(4)
    queries[(1 - zh) * X + x] = keys[block(Y, zl)]
    for c in every:
        along_x(1, c)
    for c in every:
        along_y_again(2, c)
    for c in every:
        far_arrived(0, c)
    picks_arrived(1)
    picks_along(2)
    prepare(0)
    for c in every:
        along_y_again(3, c)
    for c in every:
        far_arrived(1, c)
    picks_arrived(2)
    picks_along(3)
    for c in every:
        far_arrived(2, c)
    prepare(1)

    for made in local[3:]:
        made.wait()

    band = []
    for t in range(ROUNDS):
        index = jnp.full((1, DRAWS), bands[t], jnp.int32).astype(jnp.float32)
        band.append((D / 32.0) * (1.0 + index / 256.0))
    for c in every:
        far_arrived(3, c)
    for made in sib_copies:
        made.wait_recv()

    picks_arrived(3)
    picks_along(4)
    l_copies = []
    for n, m in enumerate((x_far, x_up, x_down, x)):
        shift = query_half[m, 0:1]
        for first in range(0, PAIRS, SLOTS):
            rows = []
            for s in range(first, first + SLOTS):
                p = table[m, s]
                rows.append(keys[lax.div(p, SUBS), lax.rem(p, SUBS)])
            rows = jnp.concatenate(rows, 0)
            norm_half = 0.5 * jnp.sum(rows * rows, -1, keepdims=True)
            key_high, key_low = split(rows)
            product = nt_dot(jnp.concatenate([key_high, key_low, key_high], 1), parts[m])
            value = (product - norm_half).reshape(SLOTS, ROWS, DRAWS)
            peak = jnp.max(value, 1, keepdims=True)
            value = value - peak
            peak = peak.reshape(SLOTS, DRAWS) - shift
            for t in range(ROUNDS):
                rate = LOG2E / band[t]
                mass = jnp.sum(jnp.exp2(value * rate[None]), 1)
                sums_out[m, t, pl.ds(first, SLOTS)] = peak * rate + jnp.log2(mass)
        if n < X - 1:
            l_copies.append(go(copy(sums_out.at[m], sums_in.at[n], l_send.at[n], l_recv.at[n], x=m)))
        else:
            sums_in[n] = sums_out[m]

    for made in l_copies:
        made.wait_recv()
    pair_out[...] = log_sum(sums_in[...])
    pair_copy = go(copy(pair_out, pair_in, pair_send, pair_recv, zh=1 - zh))
    spread = []
    picks_arrived(4)
    for t in range(ROUNDS):
        centre = jnp.concatenate([pick_out[5, 2 * t : 2 * t + 1], pick_out[5, 2 * t + 1 : 2 * t + 2]], 1)
        away = queries[:, x].reshape(DRAWS, D) - centre / MEMBERS
        spread.append(row_sums(away * away) / (2.0 * band[t]))
    while sends[0] is not pair_copy:
        sends.pop(0).wait_send()
    for k in range(ZL):
        for c in every:
            z_onward(k, c, lambda made: made.wait_send())
        if k:
            relay_onward(k, lambda made: made.wait_send(), False)
    pair_copy.wait_recv()
    first, second = pair_out[...], pair_in[...]
    peak = jnp.maximum(first, second)
    whole = peak + jnp.log2(jnp.exp2(first - peak) + jnp.exp2(second - peak))
    for t in range(ROUNDS):
        logits = (LN2 / PAIRS) * jnp.sum(whole[t], 0, keepdims=True) - spread[t]
        logits = logits - jnp.max(logits, -1, keepdims=True)
        result = logits - jnp.log(jnp.sum(jnp.exp(logits), -1, keepdims=True))
        result = jnp.where(zh == 0, result[:, : X * ROWS], result[:, X * ROWS :])
        for k in range(X):
            final_out[k, t : t + 1, 0:ROWS] = result[:, k * ROWS : (k + 1) * ROWS]
    f_copies = []
    for n, k in enumerate((x_far, x_up, x_down)):
        f_copies.append(go(copy(final_out.at[k], final_in.at[x], f_send.at[n], f_recv.at[n], x=k)))
    final_in[x] = final_out[x]
    for made in f_copies:
        made.wait_recv()
    for m in range(SUBS):
        out[:, m] = final_in[m, 0:ROUNDS, 0:ROWS]
    for made in sends:
        made.wait_send()


def per_device(samples, pair_table, assignment, band_index):
    dma = pltpu.SemaphoreType.DMA
    hbm = pl.BlockSpec(memory_space=pltpu.HBM)
    vmem = pl.BlockSpec(memory_space=pltpu.VMEM)
    f32 = jnp.float32
    siblings = 1 + (Y * ZL - 1) * PIECES
    return pl.pallas_call(
        kernel,
        name="weights",
        out_shape=jax.ShapeDtypeStruct((ROUNDS, SUBS, ROWS), f32),
        in_specs=[hbm] * 4,
        out_specs=vmem,
        scratch_shapes=[
            pltpu.SMEM((SUBS, PAIRS), jnp.int32),
            pltpu.SMEM((ROUNDS, SUBS), jnp.int32),
            pltpu.SMEM((ROUNDS,), jnp.int32),
            pltpu.VMEM(((Y + 1) * ZL * CORES, SUBS, ROWS, D), f32),
            pltpu.VMEM((GROUP, SUBS, ROWS, D), f32),
            pltpu.VMEM((SUBS, DRAWS, 3 * D), jnp.bfloat16),
            pltpu.VMEM((SUBS, 8, DRAWS), f32),
            pltpu.VMEM((SUBS, ROUNDS, PAIRS, DRAWS), f32),
            pltpu.VMEM((X, ROUNDS, PAIRS, DRAWS), f32),
            pltpu.VMEM((ROUNDS, PAIRS, DRAWS), f32),
            pltpu.VMEM((ROUNDS, PAIRS, DRAWS), f32),
            pltpu.VMEM((6, 8, 128), f32),
            pltpu.VMEM((5, 3, 8, 128), f32),
            pltpu.VMEM((X, 8, 128), f32),
            pltpu.VMEM((X, 8, 128), f32),
            dma((5,)),
            dma((ZL, PIECES, 2)), dma((ZL, PIECES)),
            dma((ZL, PIECES, 2)), dma((ZL, PIECES, 2)),
            dma((ZL, PIECES, 2)), dma((ZL, PIECES, 2)),
            dma((siblings,)), dma((siblings,)),
            dma((ZL, 2)), dma((ZL, 2)),
            dma((ZH, PIECES, X - 1)), dma((ZH, PIECES, X - 1)),
            dma((5, 3)), dma((5, 3)),
            dma((X - 1,)), dma((X - 1,)),
            dma, dma,
            dma((X - 1,)), dma((X - 1,)),
        ],
        compiler_params=pltpu.CompilerParams(
            collective_id=0, has_side_effects=True, vmem_limit_bytes=60 * 1024 * 1024
        ),
    )(pair_table, assignment, band_index, samples)


def solution(mesh):
    finer = Mesh(mesh.devices.reshape(Y, ZL, CORES, ZH, X), NAMES)
    blk, grp = NAMES[:3], NAMES[3:]
    return jax.shard_map(
        per_device,
        mesh=finer,
        in_specs=(P(blk, grp, None), P(blk, None), P(None, blk), P()),
        out_specs=P(None, blk, grp),
        check_vma=False,
    )
```
